32 devices in a mesh: req: 4 (over y, x), grp: 8 (over z, core).
Axes of the slice: x: 2, y: 2, z: 4, core: 2. Of those that a mesh axis runs over, the one named last changes fastest.
Arguments:
- item_table: bfloat16 [32768, 512], P('grp'), may hold values from -6 to 6
- cand_owner: int32 [4, 8192, 1], P('req', 'grp'), may hold values from 0 to 7; in each aligned block of 1024 rows (0 to 1023, 1024 to 2047, ..., all dimensions but the last counted through in order) at most 128 rows name the same one
- cand_row: int32 [4, 8192], P('req', 'grp'), may hold values from 0 to 4095
- hist_kv: bfloat16 [2, 4, 2048, 1024], P(None, 'req', 'grp'), may hold values from -6 to 6
- hist_len: int32 [4], P('req'), may hold values from 512 to 2048, as said below
- w_in: bfloat16 [2, 512, 1024], replicated, may hold values from -0.25 to 0.25
- w_out: bfloat16 [2, 512, 512], replicated, may hold values from -0.25 to 0.25
Outputs:
- candidate_states: bfloat16 [4, 8192, 512], P('req', 'grp')
The draws below stay inside these ranges and needn't reach their ends.
Inputs may be any that keep to these rules, and one draw needn't show every extreme that they name: `cand_owner`: among the 1024 candidates of one device, at most 128 name the same block, and some block is named exactly 128 times. `hist_len`: some request has all 2048 events live.
All inputs are finite; a program needn't handle non-finite values.
Results may differ from the reference program's by a relative error of at most 0.0085.
Values may be sent and summed in bfloat16 or wider, within the bound.
A program may use at most 128 MiB of HBM per device.

```python
import math
import jax
import jax.numpy as jnp
import numpy as np
from jax import lax

D = 512
HEADS = 4
HEAD = 128
LAYERS = 2
CAND_DEV = 1024
ITEMS_DEV = 4096
MOST = 128
REQS = 4
CAND = 8192
HIST = 2048
ITEMS = 32768
N_GRP = 8


def draw_hist_len(key, part):
    first_key, second_key = jax.random.split(jax.random.fold_in(key, 11))
    lengths = jax.random.randint(first_key, (REQS,), HIST // 4, HIST + 1)
    chosen = jax.random.randint(second_key, (), 0, REQS)
    return jnp.where(jnp.arange(REQS) == chosen, HIST, lengths).astype(jnp.int32)


def set_ends(entries, own_key, least, top_value):
    longest = entries.shape.index(max(entries.shape))
    spots = []
    for shift in (0, 1):
        where = [jax.random.randint(jax.random.fold_in(own_key, axis), (), 0, length) for axis, length in enumerate(entries.shape)]
        where[longest] = (where[longest] + shift) % entries.shape[longest]
        spots.append(tuple(where))
    return entries.at[spots[0]].set(least).at[spots[1]].set(top_value)


def block_levels(stream_key, dims, pieces, least, largest):
    level, own = 1.0, jax.random.fold_in(stream_key, 6)
    for axis_at, blocks in pieces:
        draws = jnp.exp(jax.random.uniform(jax.random.fold_in(own, axis_at), (blocks,), jnp.float32, least / len(pieces), largest / len(pieces)))
        level = level * jnp.repeat(draws, dims[axis_at] // blocks).reshape([-1 if axis == axis_at else 1 for axis in range(len(dims))])
    return level


def assign_block(own_key, own, number, rows, amount, top, most, lean):
    ranking = jax.random.permutation(own_key, amount)
    heavy_load, usual = shares(amount, rows * top, most, lean, True), shares(amount, rows * top, most, lean, False)
    places = jnp.arange(amount)

    def named(tallies, turn):
        used = int((tallies > 0).sum())
        fixed = max(1, used // 4)
        moved = fixed + (places - fixed + turn * (used - fixed)) % max(1, amount - fixed)
        return jnp.zeros((amount,), jnp.int32).at[ranking[jnp.where(places < fixed, places, moved)]].set(jnp.asarray(tallies, jnp.int32))

    tallies = jnp.where(number % 4 == 0, named(heavy_load, number // 4), named(usual, number - number // 4 - 1))
    mixed = jax.random.permutation(jax.random.fold_in(own, 3), amount)
    source_of, sink = mixed[0:amount // 2 * 2:2], mixed[1:amount // 2 * 2:2]
    slack = jnp.minimum(tallies[source_of] - 1, most - tallies[sink]) // 2
    slack = jnp.where((source_of == ranking[0]) | (sink == ranking[0]) | (tallies[sink] == 0), 0, jnp.maximum(slack, 0))
    moved = jax.random.randint(jax.random.fold_in(own, 4), (amount // 2,), 0, 1 << 20) % (slack + 1)
    tallies = tallies.at[source_of].add(-moved).at[sink].add(moved)
    labels = jnp.searchsorted(jnp.cumsum(tallies), jnp.arange(rows * top), side="right").astype(jnp.int32)
    listing = labels.reshape(top, rows).T
    listing = listing[jax.random.permutation(jax.random.fold_in(own, 1), rows)]
    turn = jax.random.randint(jax.random.fold_in(own, 2), (rows, 1), 0, top)
    return jnp.take_along_axis(listing, (jnp.arange(top)[None, :] + turn) % top, axis=1)


def shares(count, total, reach, skew, full):
    portions = [(1 << 20) // math.isqrt(rank ** skew) + 1 for rank in range(1, count + 1)]
    largest = reach if full else min(reach, max(-(-total // count), total * portions[0] // sum(portions)))
    least = 1 if total - largest >= count - 1 else 0
    holding, surplus = [largest] + [least] * (count - 1), total - largest - least * (count - 1)
    while surplus > 0:
        candidates = [i for i in range(1, count) if holding[i] < largest] or [i for i in range(1, count) if holding[i] < reach]
        whole, budget = sum([portions[i] for i in candidates]), surplus
        for i in candidates:
            extra = min(reach - holding[i], max(1, budget * portions[i] // whole), surplus)
            holding[i] = holding[i] + extra
            surplus = surplus - extra
    return np.array(holding)


def normal_values(stream_key, extent, width, limit, pieces=(), kind=jnp.bfloat16):
    drawn = jax.random.normal(stream_key, extent, jnp.float32) * width
    if len(pieces) > 0:
        drawn = block_levels(stream_key, extent, pieces, -0.22, 0.18) * drawn
    return jnp.clip(drawn, min=-limit, max=limit).astype(kind)


def setup_inputs(seed: int = 0) -> dict:
    keys = jax.random.split(jax.random.key(seed), 8)
    item_table = normal_values(keys[0], (ITEMS, D), 1.0, 6.0, ((0, 8),))
    cand_owner_keys = jax.random.split(jax.random.fold_in(keys[1], 1), REQS * CAND // CAND_DEV)
    cand_owner_turns = jax.random.permutation(jax.random.fold_in(keys[1], 3), REQS * CAND // CAND_DEV)
    cand_owner = jax.vmap(lambda own, number: assign_block(jax.random.fold_in(keys[1], 2), own, number, CAND_DEV, N_GRP, 1, MOST, 2))(cand_owner_keys, cand_owner_turns).reshape((REQS, CAND, 1))
    cand_row = set_ends(jax.random.randint(keys[2], (REQS, CAND), 0, ITEMS_DEV), jax.random.fold_in(keys[2], 1), 0, ITEMS_DEV - 1).astype(jnp.int32)
    hist_kv = normal_values(keys[3], (LAYERS, REQS, HIST, 2 * D), 1.0, 6.0, ((1, 4), (2, 8)))
    hist_len = draw_hist_len(jax.random.fold_in(keys[7], 71), 0)
    w_in = normal_values(keys[5], (LAYERS, D, 2 * D), D ** -0.5, 0.25)
    w_out = normal_values(keys[6], (LAYERS, D, D), D ** -0.5, 0.25)
    return {"item_table": item_table, "cand_owner": cand_owner, "cand_row": cand_row, "hist_kv": hist_kv, "hist_len": hist_len, "w_in": w_in, "w_out": w_out}


score_scale = 0.35
epsilon = 1e-05

def normalize(values):
    center = values - lax.optimization_barrier(jnp.mean(values, axis=-1, keepdims=True))
    return center * lax.rsqrt(lax.optimization_barrier(jnp.mean(center * center, axis=-1, keepdims=True)) + epsilon)

def ref_layer(rows_now, cache_rows, length, weight_in, weight_out):
    normed = normalize(rows_now.astype(jnp.float32)).astype(jnp.bfloat16)
    projected = jax.nn.silu(jnp.dot(normed, weight_in, preferred_element_type=jnp.float32))
    gate_vals = projected[:, :D]
    queries = projected[:, D:].astype(jnp.bfloat16)
    key_rows = cache_rows[:, :D].reshape(HIST, HEADS, HEAD).astype(jnp.float32)
    value_rows = cache_rows[:, D:].reshape(HIST, HEADS, HEAD).astype(jnp.float32)
    live = jnp.arange(HIST, dtype=jnp.int32) < length
    block_rows = math.gcd(CAND, 1024)
    blocks = queries.reshape(CAND // block_rows, block_rows, HEADS, HEAD)

    def one_block(query_block):
        scores = jnp.einsum('chd,khd->hck', query_block.astype(jnp.float32), key_rows) * score_scale
        weights = jnp.where(live[None, None, :], jax.nn.silu(scores), 0.0).astype(jnp.bfloat16)
        attended = jnp.einsum('hck,khd->chd', weights.astype(jnp.float32), value_rows)
        return attended.reshape(block_rows, D)
    attended = lax.map(one_block, blocks).reshape(CAND, D)
    hidden = (normalize(attended) * gate_vals).astype(jnp.bfloat16)
    return (rows_now.astype(jnp.float32) + jnp.dot(hidden, weight_out, preferred_element_type=jnp.float32)).astype(jnp.bfloat16)

def reference(item_table, cand_owner, cand_row, hist_kv, hist_len, w_in, w_out):
    item_ids = (cand_owner[:, :, 0] * ITEMS_DEV + cand_row).astype(jnp.int32)
    outputs = []
    for request in range(REQS):
        rows_now = jnp.take(item_table, item_ids[request], axis=0)
        for layer_index in range(LAYERS):
            rows_now = ref_layer(rows_now, hist_kv[layer_index, request], hist_len[request], w_in[layer_index], w_out[layer_index])
        outputs.append(rows_now)
    return jnp.stack(outputs)
```

```python
from functools import partial

import jax
import jax.numpy as jnp
from jax import lax
from jax.experimental import pallas as pl
from jax.experimental.pallas import tpu as pltpu
from jax.sharding import PartitionSpec as P

D = 512
HEADS = 4
HEAD = 128
LAYERS = 2
MOST = 128
MESH = pl.DeviceIdType.MESH

score_scale = 0.35
epsilon = 1e-05


def normalize(values):
    center = values - jnp.mean(values, axis=-1, keepdims=True)
    return center * lax.rsqrt(jnp.mean(center * center, axis=-1, keepdims=True) + epsilon)


def silu_of_twice(half):
    return half + half * jnp.tanh(half)


def kernel(
    groups,
    len_ref, owner_ref, row_ref, table_ref, hist_ref, w_in_ref, w_out_ref, out_ref,
    kv, place, asked, wanted, found, returned, rows_now, queries, gate, summed, live_values,
    own_sem, z_recv, s_recv, r_send, l_send, s_send, ask_send, ask_recv, back_send, back_recv,
):
    chips = groups // 2
    me = lax.axis_index("grp")
    pos, core = me // 2, me % 2
    sibling = 2 * pos + 1 - core
    cands = rows_now.shape[0]
    items = table_ref.shape[0]
    hist_rows = hist_ref.shape[1]
    tile = 256
    f32, bf16 = jnp.float32, jnp.bfloat16

    barrier = pltpu.get_barrier_semaphore()

    @pl.loop(1, groups)
    def _(k):
        pl.semaphore_signal(
            barrier, inc=1, device_id={"grp": (me + k) % groups}, device_id_type=MESH
        )

    own_copies = [
        pltpu.make_async_copy(hist_ref.at[layer], kv.at[layer, me], own_sem.at[layer])
        for layer in range(LAYERS)
    ]
    for copy in own_copies:
        copy.start()
    pl.semaphore_wait(barrier, groups - 1)

    def push(layer, chip, lane, target, send, recv):
        block = kv.at[layer, 2 * chip + lane]
        return pltpu.make_async_remote_copy(
            src_ref=block, dst_ref=block, send_sem=send.at[layer, chip],
            recv_sem=recv.at[layer, chip], device_id={"grp": target}, device_id_type=MESH,
        )

    def to_right(layer, chip):
        return push(layer, chip, core, me + 2, r_send, z_recv)

    def to_left(layer, chip):
        return push(layer, chip, core, me - 2, l_send, z_recv)

    def to_sibling(layer, chip):
        return push(layer, chip, core, sibling, s_send, s_recv)

    def from_sibling(layer, chip):
        return push(layer, chip, 1 - core, sibling, s_send, s_recv)

    def goes_right(chip):
        return jnp.logical_and(chip <= pos, pos + 1 < chips)

    def goes_left(chip):
        return jnp.logical_and(chip >= pos, pos > 0)

    def pass_on(layer, chip):
        @pl.when(goes_right(chip))
        def _():
            to_right(layer, chip).start()

        @pl.when(goes_left(chip))
        def _():
            to_left(layer, chip).start()

        to_sibling(layer, chip).start()

    def at_distance(distance, act):
        @pl.loop(0, 2)
        def _(side):
            chip = pos + (2 * side - 1) * distance

            @pl.when(jnp.logical_and(chip >= 0, chip < chips))
            def _():
                act(chip)

    def relay(layer, distance):
        def act(chip):
            to_right(layer, chip).wait_recv()
            pass_on(layer, chip)

        at_distance(distance, act)

    own_copies[0].wait()
    pass_on(0, pos)

    owners = owner_ref[...]
    names = (owners == lax.broadcasted_iota(jnp.int32, (cands, 128), 1)).astype(f32)
    names16 = names.astype(bf16)
    for start in range(0, cands, tile):
        earlier = (
            lax.broadcasted_iota(jnp.int32, (tile, cands), 1)
            < start + lax.broadcasted_iota(jnp.int32, (tile, cands), 0)
        ).astype(f32).astype(bf16)
        rank = jnp.dot(earlier, names16, preferred_element_type=f32)
        own_rank = jnp.sum(rank * names[start : start + tile], axis=1, keepdims=True)
        flat = owners[start : start + tile] * MOST + own_rank.astype(jnp.int32)
        place[start : start + tile, :] = (
            (flat == lax.broadcasted_iota(jnp.int32, (tile, groups * MOST), 1))
            .astype(f32)
            .astype(bf16)
        )
    item_rows = row_ref[...]
    high = (item_rows >> 6).astype(f32)
    low = (item_rows & 63).astype(f32)
    halves = jnp.concatenate([high, low, jnp.zeros((6, cands), f32)], axis=0).astype(bf16)
    listed = jnp.dot(halves, place[...], preferred_element_type=f32)
    requested = (listed[0:1] * 64.0 + listed[1:2]).astype(jnp.int32)
    for owner in range(groups):
        asked[owner] = requested[:, owner * MOST : (owner + 1) * MOST]

    def ask(peer, slot):
        return pltpu.make_async_remote_copy(
            src_ref=asked.at[peer], dst_ref=wanted.at[slot], send_sem=ask_send.at[peer],
            recv_sem=ask_recv.at[slot], device_id={"grp": peer}, device_id_type=MESH,
        )

    def give_back(peer, slot):
        return pltpu.make_async_remote_copy(
            src_ref=found.at[peer], dst_ref=returned.at[slot], send_sem=back_send.at[peer],
            recv_sem=back_recv.at[slot], device_id={"grp": peer}, device_id_type=MESH,
        )

    @pl.loop(1, groups)
    def _(k):
        ask((me + k) % groups, me).start()

    wanted[me] = asked[me]

    @pl.loop(1, groups)
    def _(k):
        peer = (me + k) % groups
        ask(peer, peer).wait_recv()

    at_once = 4
    chunk = 512

    @pl.loop(0, groups // at_once)
    def _(batch):
        columns = []
        for k in range(at_once):
            line = wanted[batch * at_once + k].astype(f32)
            columns.append(jnp.broadcast_to(line, (MOST, MOST)).T[:, 0:1].astype(jnp.int32))
        column = jnp.concatenate(columns, axis=0)
        total = jnp.zeros((at_once * MOST, D), f32)
        for start in range(0, items, chunk):
            picks = (
                column
                == start + lax.broadcasted_iota(jnp.int32, (at_once * MOST, chunk), 1)
            ).astype(f32).astype(bf16)
            total += jnp.dot(
                picks, table_ref[start : start + chunk, :], preferred_element_type=f32
            )
        found[pl.ds(batch * at_once, at_once)] = total.astype(bf16).reshape(at_once, MOST, D)

        @pl.loop(0, at_once)
        def _(k):
            peer = batch * at_once + k

            @pl.when(peer != me)
            def _():
                give_back(peer, me).start()

    returned[me] = found[me]
    relay(0, 1)

    @pl.loop(1, groups)
    def _(k):
        peer = (me + k) % groups
        give_back(peer, peer).wait_recv()

    def project(layer, start, rows):
        normed = normalize(rows.astype(f32)).astype(bf16)
        projected = silu_of_twice(
            0.5 * jnp.dot(normed, w_in_ref[layer], preferred_element_type=f32)
        )
        gate[pl.ds(start, tile), :] = projected[:, :D]
        queries[pl.ds(start, tile), :] = projected[:, D:].astype(bf16)
        summed[pl.ds(start, tile), :] = jnp.zeros((tile, D), f32)

    @pl.loop(0, cands // tile)
    def _(step):
        start = pl.multiple_of(step * tile, tile)
        rows = jnp.dot(
            place[pl.ds(start, tile), :],
            returned[...].reshape(groups * MOST, D),
            preferred_element_type=f32,
        ).astype(bf16)
        rows_now[pl.ds(start, tile), :] = rows
        project(0, start, rows)

    length = len_ref[0]

    def attend(layer, chip):
        from_sibling(layer, chip).wait_recv()
        for lane in range(2):
            position = (2 * chip + lane) * hist_rows + lax.broadcasted_iota(
                jnp.int32, (hist_rows, D), 0
            )
            values = kv[layer, 2 * chip + lane, :, D:].astype(f32)
            live_values[lane * hist_rows : (lane + 1) * hist_rows, :] = jnp.where(
                position < length, values, 0.0
            ).astype(bf16)

        @pl.loop(0, cands // tile)
        def _(step):
            start = pl.multiple_of(step * tile, tile)
            for head in range(HEADS):
                part = slice(head * HEAD, (head + 1) * HEAD)
                keys = kv[layer, pl.ds(2 * chip, 2), :, part].reshape(2 * hist_rows, HEAD)
                scores = lax.dot_general(
                    queries[pl.ds(start, tile), part], keys, (((1,), (1,)), ((), ())),
                    preferred_element_type=f32,
                )
                weights = silu_of_twice(scores * (0.5 * score_scale)).astype(bf16)
                summed[pl.ds(start, tile), part] += jnp.dot(
                    weights, live_values[:, part], preferred_element_type=f32
                )

    def finish(layer):
        @pl.loop(0, cands // tile)
        def _(step):
            start = pl.multiple_of(step * tile, tile)
            here = pl.ds(start, tile)
            hidden = (normalize(summed[here, :]) * gate[here, :]).astype(bf16)
            rows = (
                rows_now[here, :].astype(f32)
                + jnp.dot(hidden, w_out_ref[layer], preferred_element_type=f32)
            ).astype(bf16)
            if layer + 1 < LAYERS:
                rows_now[here, :] = rows
                project(layer + 1, start, rows)
            else:
                out_ref[here, :] = rows

    own_copies[1].wait()
    attend(0, pos)
    for distance in range(1, chips):
        if distance + 1 < chips:
            relay(0, distance + 1)
        if distance == max(chips - 3, 1):
            pass_on(1, pos)
        at_distance(distance, partial(attend, 0))
    if chips > 1:
        relay(1, 1)
    finish(0)
    attend(1, pos)
    for distance in range(1, chips):
        if distance + 1 < chips:
            relay(1, distance + 1)
        at_distance(distance, partial(attend, 1))
    finish(1)

    for layer in range(LAYERS):
        @pl.loop(0, chips)
        def _(chip):
            @pl.when(goes_right(chip))
            def _():
                to_right(layer, chip).wait_send()

            @pl.when(goes_left(chip))
            def _():
                to_left(layer, chip).wait_send()

            to_sibling(layer, chip).wait_send()

    @pl.loop(1, groups)
    def _(k):
        peer = (me + k) % groups
        ask(peer, peer).wait_send()
        give_back(peer, peer).wait_send()


def body(item_table, cand_owner, cand_row, hist_kv, hist_len, w_in, w_out):
    groups = lax.axis_size("grp")
    cands = cand_row.shape[1]
    hist_rows = hist_kv.shape[2]
    vmem = pl.BlockSpec(memory_space=pltpu.VMEM)
    dma, f32, bf16 = pltpu.SemaphoreType.DMA, jnp.float32, jnp.bfloat16
    chips = groups // 2
    rows = pl.pallas_call(
        partial(kernel, groups),
        out_shape=jax.ShapeDtypeStruct((cands, D), bf16),
        in_specs=[
            pl.BlockSpec(memory_space=pltpu.SMEM), vmem, vmem, vmem,
            pl.BlockSpec(memory_space=pl.ANY), vmem, vmem,
        ],
        out_specs=vmem,
        scratch_shapes=[
            pltpu.VMEM((LAYERS, groups, hist_rows, 2 * D), bf16),
            pltpu.VMEM((cands, groups * MOST), bf16),
            pltpu.VMEM((groups, 1, MOST), jnp.int32),
            pltpu.VMEM((groups, 1, MOST), jnp.int32),
            pltpu.VMEM((groups, MOST, D), bf16),
            pltpu.VMEM((groups, MOST, D), bf16),
            pltpu.VMEM((cands, D), bf16),
            pltpu.VMEM((cands, D), bf16),
            pltpu.VMEM((cands, D), f32),
            pltpu.VMEM((cands, D), f32),
            pltpu.VMEM((2 * hist_rows, D), bf16),
            dma((LAYERS,)),
            dma((LAYERS, chips)),
            dma((LAYERS, chips)),
            dma((LAYERS, chips)),
            dma((LAYERS, chips)),
            dma((LAYERS, chips)),
            dma((groups,)),
            dma((groups,)),
            dma((groups,)),
            dma((groups,)),
        ],
        compiler_params=pltpu.CompilerParams(
            collective_id=0, has_side_effects=True, vmem_limit_bytes=56 * 1024 * 1024
        ),
    )(hist_len, cand_owner[0], cand_row, item_table, hist_kv[:, 0], w_in, w_out)
    return rows[None]


def solution(mesh):
    in_specs = (
        P("grp", None),
        P("req", "grp", None),
        P("req", "grp"),
        P(None, "req", "grp", None),
        P("req"),
        P(),
        P(),
    )
    out_specs = P("req", "grp", None)
    return jax.shard_map(body, mesh=mesh, in_specs=in_specs, out_specs=out_specs, check_vma=False)
```

```python
from functools import partial

import jax
import jax.numpy as jnp
from jax import lax
from jax.experimental import pallas as pl
from jax.experimental.pallas import tpu as pltpu
from jax.sharding import PartitionSpec as P

D = 512
HEADS = 4
HEAD = 128
LAYERS = 2
MOST = 128
PARTS = 1
MESH = pl.DeviceIdType.MESH

score_scale = 0.35
epsilon = 1e-05


def normalize(values):
    center = values - jnp.mean(values, axis=-1, keepdims=True)
    return center * lax.rsqrt(jnp.mean(center * center, axis=-1, keepdims=True) + epsilon)


def silu_of_twice(half):
    return half + half * jnp.tanh(half)


def kernel(
    groups,
    len_ref, owner_ref, row_ref, table_hbm, hist_ref, w_in_hbm, w_out_hbm, out_ref,
    table_ref, w_in_ref, w_out_ref, kv, place, asked, wanted, found, returned, rows_now, queries, gate, summed, live_values,
    load_sem, own_sem, z_recv, s_recv, r_send, l_send, s_send, ask_send, ask_recv, back_send, back_recv,
):
    chips = groups // 2
    me = lax.axis_index("grp")
    pos, core = me // 2, me % 2
    sibling = 2 * pos + 1 - core
    cands = rows_now.shape[0]
    items = table_ref.shape[0]
    hist_rows = hist_ref.shape[1]
    tile = 256
    half = hist_rows // PARTS
    f32, bf16 = jnp.float32, jnp.bfloat16

    barrier = pltpu.get_barrier_semaphore()

    @pl.loop(1, groups)
    def _(k):
        pl.semaphore_signal(
            barrier, inc=1, device_id={"grp": (me + k) % groups}, device_id_type=MESH
        )

    own_copies = [
        pltpu.make_async_copy(hist_ref.at[layer], kv.at[layer, me], own_sem.at[layer])
        for layer in range(LAYERS)
    ]
    loads = [
        pltpu.make_async_copy(far, near, load_sem.at[index])
        for index, (far, near) in enumerate(
            [(table_hbm, table_ref), (w_in_hbm, w_in_ref), (w_out_hbm, w_out_ref)]
        )
    ]
    for copy in own_copies + loads:
        copy.start()
    pl.semaphore_wait(barrier, groups - 1)

    def push(layer, chip, lane, part, target, send, recv):
        block = kv.at[layer, 2 * chip + lane, pl.ds(part * half, half)]
        return pltpu.make_async_remote_copy(
            src_ref=block, dst_ref=block, send_sem=send.at[layer, chip, part],
            recv_sem=recv.at[layer, chip, part], device_id={"grp": target}, device_id_type=MESH,
        )

    def to_right(layer, chip, part):
        return push(layer, chip, core, part, me + 2, r_send, z_recv)

    def to_left(layer, chip, part):
        return push(layer, chip, core, part, me - 2, l_send, z_recv)

    def to_sibling(layer, chip, part):
        return push(layer, chip, core, part, sibling, s_send, s_recv)

    def from_sibling(layer, chip, part):
        return push(layer, chip, 1 - core, part, sibling, s_send, s_recv)

    def goes_right(chip):
        return jnp.logical_and(chip <= pos, pos + 1 < chips)

    def goes_left(chip):
        return jnp.logical_and(chip >= pos, pos > 0)

    def pass_on(layer, chip, part):
        @pl.when(goes_right(chip))
        def _():
            to_right(layer, chip, part).start()

        @pl.when(goes_left(chip))
        def _():
            to_left(layer, chip, part).start()

        to_sibling(layer, chip, part).start()

    def at_distance(distance, act):
        @pl.loop(0, 2)
        def _(side):
            chip = pos + (2 * side - 1) * distance

            @pl.when(jnp.logical_and(chip >= 0, chip < chips))
            def _():
                act(chip)

    interior = jnp.logical_and(pos > 0, pos + 1 < chips)
    emitted = set()

    def relay(layer, distance, inner, parts=range(PARTS)):
        parts = [part for part in parts if (layer, distance, inner, part) not in emitted]
        if distance >= chips or not parts:
            return
        emitted.update((layer, distance, inner, part) for part in parts)

        def act(chip):
            for part in parts:
                to_right(layer, chip, part).wait_recv()
                pass_on(layer, chip, part)

        @pl.when(interior if inner else jnp.logical_not(interior))
        def _():
            at_distance(distance, act)

    own_copies[0].wait()
    for part in range(PARTS):
        pass_on(0, pos, part)

    owners = jnp.concatenate(
        [
            jnp.broadcast_to(owner_ref[:, start : start + 128].astype(f32), (128, 128)).T[:, 0:1]
            for start in range(0, cands, 128)
        ],
        axis=0,
    ).astype(jnp.int32)
    names = (owners == lax.broadcasted_iota(jnp.int32, (cands, 128), 1)).astype(f32)
    names16 = names.astype(bf16)
    for start in range(0, cands, tile):
        earlier = (
            lax.broadcasted_iota(jnp.int32, (tile, cands), 1)
            < start + lax.broadcasted_iota(jnp.int32, (tile, cands), 0)
        ).astype(f32).astype(bf16)
        rank = jnp.dot(earlier, names16, preferred_element_type=f32)
        own_rank = jnp.sum(rank * names[start : start + tile], axis=1, keepdims=True)
        flat = owners[start : start + tile] * MOST + own_rank.astype(jnp.int32)
        place[start : start + tile, :] = (
            (flat == lax.broadcasted_iota(jnp.int32, (tile, groups * MOST), 1))
            .astype(f32)
            .astype(bf16)
        )
    item_rows = row_ref[...]
    high = (item_rows >> 6).astype(f32)
    low = (item_rows & 63).astype(f32)
    halves = jnp.concatenate([high, low, jnp.zeros((6, cands), f32)], axis=0).astype(bf16)
    listed = jnp.dot(halves, place[...], preferred_element_type=f32)
    requested = (listed[0:1] * 64.0 + listed[1:2]).astype(jnp.int32)
    for owner in range(groups):
        asked[owner] = requested[:, owner * MOST : (owner + 1) * MOST]

    def ask(peer, slot):
        return pltpu.make_async_remote_copy(
            src_ref=asked.at[peer], dst_ref=wanted.at[slot], send_sem=ask_send.at[peer],
            recv_sem=ask_recv.at[slot], device_id={"grp": peer}, device_id_type=MESH,
        )

    def give_back(peer, slot):
        return pltpu.make_async_remote_copy(
            src_ref=found.at[peer], dst_ref=returned.at[slot], send_sem=back_send.at[peer],
            recv_sem=back_recv.at[slot], device_id={"grp": peer}, device_id_type=MESH,
        )

    @pl.loop(1, groups)
    def _(k):
        ask((me + k) % groups, me).start()

    wanted[me] = asked[me]

    @pl.loop(1, groups)
    def _(k):
        peer = (me + k) % groups
        ask(peer, peer).wait_recv()

    at_once = 4
    chunk = 512

    def gather(batch):
        columns = []
        for k in range(at_once):
            line = wanted[batch * at_once + k].astype(f32)
            columns.append(jnp.broadcast_to(line, (MOST, MOST)).T[:, 0:1].astype(jnp.int32))
        column = jnp.concatenate(columns, axis=0)
        total = jnp.zeros((at_once * MOST, D), f32)
        for start in range(0, items, chunk):
            picks = (
                column
                == start + lax.broadcasted_iota(jnp.int32, (at_once * MOST, chunk), 1)
            ).astype(f32).astype(bf16)
            total += jnp.dot(
                picks, table_ref[start : start + chunk, :], preferred_element_type=f32
            )
        found[pl.ds(batch * at_once, at_once)] = total.astype(bf16).reshape(at_once, MOST, D)

        @pl.loop(0, at_once)
        def _(k):
            peer = batch * at_once + k

            @pl.when(peer != me)
            def _():
                give_back(peer, me).start()

    loads[0].wait()
    for batch in range(groups // at_once):
        gather(batch)
        if batch == 0:
            relay(0, 1, True)
    returned[me] = found[me]
    own_copies[1].wait()
    for part in range(PARTS):
        pass_on(1, pos, part)
    relay(0, 2, True)
    loads[1].wait()
    loads[2].wait()

    @pl.loop(1, groups)
    def _(k):
        peer = (me + k) % groups
        give_back(peer, peer).wait_recv()

    def project(layer, start, rows):
        normed = normalize(rows.astype(f32)).astype(bf16)
        projected = silu_of_twice(
            0.5 * jnp.dot(normed, w_in_ref[layer], preferred_element_type=f32)
        )
        gate[pl.ds(start, tile), :] = projected[:, :D]
        queries[pl.ds(start, tile), :] = projected[:, D:].astype(bf16)
        summed[pl.ds(start, tile), :] = jnp.zeros((tile, D), f32)

    @pl.loop(0, cands // tile)
    def _(step):
        start = pl.multiple_of(step * tile, tile)
        rows = jnp.dot(
            place[pl.ds(start, tile), :],
            returned[...].reshape(groups * MOST, D),
            preferred_element_type=f32,
        ).astype(bf16)
        rows_now[pl.ds(start, tile), :] = rows
        project(0, start, rows)

    length = len_ref[0]

    def attend(layer, chip, parts=range(PARTS)):
        for part in parts:
            from_sibling(layer, chip, part).wait_recv()
        first, size = parts[0] * half, len(parts) * half
        for lane in range(2):
            position = (2 * chip + lane) * hist_rows + first + lax.broadcasted_iota(
                jnp.int32, (size, D), 0
            )
            values = kv[layer, 2 * chip + lane, first : first + size, D:].astype(f32)
            live_values[lane * size : (lane + 1) * size, :] = jnp.where(
                position < length, values, 0.0
            ).astype(bf16)

        @pl.loop(0, cands // tile)
        def _(step):
            start = pl.multiple_of(step * tile, tile)
            for head in range(HEADS):
                cols = slice(head * HEAD, (head + 1) * HEAD)
                keys = kv[
                    layer, pl.ds(2 * chip, 2), first : first + size, cols
                ].reshape(2 * size, HEAD)
                scores = lax.dot_general(
                    queries[pl.ds(start, tile), cols], keys, (((1,), (1,)), ((), ())),
                    preferred_element_type=f32,
                )
                weights = silu_of_twice(scores * (0.5 * score_scale)).astype(bf16)
                summed[pl.ds(start, tile), cols] += jnp.dot(
                    weights, live_values[: 2 * size, cols], preferred_element_type=f32
                )

    def finish(layer):
        @pl.loop(0, cands // tile)
        def _(step):
            start = pl.multiple_of(step * tile, tile)
            here = pl.ds(start, tile)
            hidden = (normalize(summed[here, :]) * gate[here, :]).astype(bf16)
            rows = (
                rows_now[here, :].astype(f32)
                + jnp.dot(hidden, w_out_ref[layer], preferred_element_type=f32)
            ).astype(bf16)
            if layer + 1 < LAYERS:
                rows_now[here, :] = rows
                project(layer + 1, start, rows)
            else:
                out_ref[here, :] = rows

    relay(0, 1, False)
    attend(0, pos)
    for distance in range(1, chips):
        relay(0, distance + 1, True)
        relay(0, distance + 1, False)
        relay(1, distance, True)
        at_distance(distance, partial(attend, 0))
    relay(1, 1, False)
    finish(0)
    attend(1, pos)
    for distance in range(1, chips):
        relay(1, distance + 1, True)
        if distance + 1 < chips - 1:
            relay(1, distance + 1, False)
        if distance < chips - 1:
            at_distance(distance, partial(attend, 1))
            continue
        for part in range(PARTS):
            relay(1, distance, False, [part])
            at_distance(distance, partial(attend, 1, parts=[part]))
    finish(1)

    for layer in range(LAYERS):
        @pl.loop(0, chips)
        def _(chip):
            for part in range(PARTS):
                @pl.when(goes_right(chip))
                def _():
                    to_right(layer, chip, part).wait_send()

                @pl.when(goes_left(chip))
                def _():
                    to_left(layer, chip, part).wait_send()

                to_sibling(layer, chip, part).wait_send()

    @pl.loop(1, groups)
    def _(k):
        peer = (me + k) % groups
        ask(peer, peer).wait_send()
        give_back(peer, peer).wait_send()


def body(item_table, cand_owner, cand_row, hist_kv, hist_len, w_in, w_out):
    groups = lax.axis_size("grp")
    cands = cand_row.shape[1]
    hist_rows = hist_kv.shape[2]
    vmem = pl.BlockSpec(memory_space=pltpu.VMEM)
    far = pl.BlockSpec(memory_space=pl.ANY)
    dma, f32, bf16 = pltpu.SemaphoreType.DMA, jnp.float32, jnp.bfloat16
    chips = groups // 2
    rows = pl.pallas_call(
        partial(kernel, groups),
        out_shape=jax.ShapeDtypeStruct((cands, D), bf16),
        in_specs=[
            pl.BlockSpec(memory_space=pltpu.SMEM), vmem, vmem, far, far, far, far,
        ],
        out_specs=vmem,
        scratch_shapes=[
            pltpu.VMEM(item_table.shape, bf16),
            pltpu.VMEM(w_in.shape, bf16),
            pltpu.VMEM(w_out.shape, bf16),
            pltpu.VMEM((LAYERS, groups, hist_rows, 2 * D), bf16),
            pltpu.VMEM((cands, groups * MOST), bf16),
            pltpu.VMEM((groups, 1, MOST), jnp.int32),
            pltpu.VMEM((groups, 1, MOST), jnp.int32),
            pltpu.VMEM((groups, MOST, D), bf16),
            pltpu.VMEM((groups, MOST, D), bf16),
            pltpu.VMEM((cands, D), bf16),
            pltpu.VMEM((cands, D), bf16),
            pltpu.VMEM((cands, D), f32),
            pltpu.VMEM((cands, D), f32),
            pltpu.VMEM((2 * hist_rows, D), bf16),
            dma((3,)),
            dma((LAYERS,)),
            dma((LAYERS, chips, PARTS)),
            dma((LAYERS, chips, PARTS)),
            dma((LAYERS, chips, PARTS)),
            dma((LAYERS, chips, PARTS)),
            dma((LAYERS, chips, PARTS)),
            dma((groups,)),
            dma((groups,)),
            dma((groups,)),
            dma((groups,)),
        ],
        compiler_params=pltpu.CompilerParams(
            collective_id=0, has_side_effects=True, vmem_limit_bytes=56 * 1024 * 1024
        ),
    )(hist_len, cand_owner[:, :, 0], cand_row, item_table, hist_kv[:, 0], w_in, w_out)
    return rows[None]


def solution(mesh):
    in_specs = (
        P("grp", None),
        P("req", "grp", None),
        P("req", "grp"),
        P(None, "req", "grp", None),
        P("req"),
        P(),
        P(),
    )
    out_specs = P("req", "grp", None)
    return jax.shard_map(body, mesh=mesh, in_specs=in_specs, out_specs=out_specs, check_vma=False)
```
